512 devices in a mesh: dop: 16 (over z, core), rng: 32 (over x, y).
Axes of the slice: x: 4, y: 8, z: 8, core: 2. Of those that a mesh axis runs over, the one named last changes fastest.
Arguments:
- cube: bfloat16 [2, 64, 128, 16384], P(None, None, 'dop', 'rng'), may hold values from -200 to 200
- train_blocks: int32 [128, 128], P('dop', 'rng'), may hold values 0 or 1
- guard_blocks: int32 [128], P('rng'), may hold values 0 or 1
- prior_factor: float32 [128, 256, 256], P('dop', 'rng'), may hold values from -1638400 to 1638400, as said below
- steering: float32 [128, 256], P('dop'), may hold values from -6 to 6
Outputs:
- filtered: float32 [2, 128, 16384], P(None, 'dop', 'rng')
- factor: float32 [128, 256, 256], P('dop', 'rng')
The draws below stay inside these ranges and needn't reach their ends.
Inputs may be any that keep to these rules, and one draw needn't show every extreme that they name: `prior_factor`: upper triangular with a positive diagonal.
All inputs are finite; a program needn't handle non-finite values. No bound on the sum of `train_blocks` or of `guard_blocks` on one device may be relied on, other than what follows from the above.
Results may differ from the reference program's by a relative error of at most 0.0041.
Values may be sent and summed in bfloat16 or wider, within the bound.
A program may use at most 64 MiB of HBM per device.

```python
import math
import jax
import jax.numpy as jnp
from jax import lax

C = 64
P_SIZE = 128
BLOCK = 128
GATES = 16384
NBLK = 128
NDOF = 256


def draw_cube(key, part):
    key_scale = jax.random.fold_in(key, 11)
    key_main = jax.random.fold_in(key, 12)
    scales = jnp.exp(jax.random.uniform(key_scale, (GATES // BLOCK,), jnp.float32, 0.0, math.log(10.0)))
    gate_scale = jnp.repeat(scales, BLOCK)
    base = jax.random.normal(key_main, (2, C, P_SIZE, GATES), jnp.float32)
    return (base * gate_scale[None, None, None, :]).astype(jnp.bfloat16)


def draw_prior_factor(key, part):
    key_diag = jax.random.fold_in(key, 21)
    key_off = jax.random.fold_in(key, 22)
    scale = 40.0 * math.sqrt(GATES)
    diagonal = jnp.exp(jax.random.uniform(key_diag, (P_SIZE, NDOF), jnp.float32, math.log(0.5), math.log(2.0)))
    off = jax.random.normal(key_off, (P_SIZE, NDOF, NDOF), jnp.float32)
    off = jnp.triu(off * (0.4 / math.sqrt(NDOF)), 1)
    upper = off + diagonal[:, :, None] * jnp.eye(NDOF, dtype=jnp.float32)[None]
    return scale * upper


def plant(result, rng, low, high):
    longest = result.shape.index(max(result.shape))
    spots = []
    for shift in (0, 1):
        where = [jax.random.randint(jax.random.fold_in(rng, axis), (), 0, length) for axis, length in enumerate(result.shape)]
        where[longest] = (where[longest] + shift) % result.shape[longest]
        spots.append(tuple(where))
    return result.at[spots[0]].set(low).at[spots[1]].set(high)


def shard_levels(stream_key, extent, cuts, low, high):
    def one(position, blocks):
        steps = jax.random.uniform(jax.random.fold_in(jax.random.fold_in(stream_key, 6), position), (blocks,), jnp.float32, low / len(cuts), high / len(cuts))
        return jnp.repeat(jnp.exp(steps), extent[position] // blocks).reshape((-1,) + (1,) * (len(extent) - position - 1))

    gain = one(*cuts[0])
    for cut in cuts[1:]:
        gain = gain * one(*cut)
    return gain


def scatter_about(stream_key, dims, scale, limit, split=(), kind=jnp.bfloat16):
    drawn = scale * jax.random.normal(stream_key, dims, jnp.float32)
    if split:
        drawn = drawn * shard_levels(stream_key, dims, split, -0.22, 0.18)
    return jnp.clip(drawn, -limit, limit).astype(kind)


def setup_inputs(seed: int = 0) -> dict:
    key_list = jax.random.split(jax.random.key(seed), 6)
    cube = draw_cube(jax.random.fold_in(key_list[5], 71), 0)
    train_blocks = plant((jax.random.randint(key_list[1], (P_SIZE, NBLK), 0, 2) < 1).astype(jnp.int32), jax.random.fold_in(key_list[1], 1), 0, 1)
    guard_blocks = plant((jax.random.randint(key_list[2], (NBLK,), 0, 4) < 3).astype(jnp.int32), jax.random.fold_in(key_list[2], 1), 0, 1)
    prior_factor = draw_prior_factor(jax.random.fold_in(key_list[5], 71), 0)
    steering = scatter_about(key_list[4], (P_SIZE, NDOF), 1.0, 6.0, ((0, 16),), jnp.float32)
    return {"cube": cube, "train_blocks": train_blocks, "guard_blocks": guard_blocks, "prior_factor": prior_factor, "steering": steering}


def one_channel(channel):
    samples = channel[0].astype(jnp.float32) + 1j * channel[1].astype(jnp.float32)
    spectra = jnp.fft.fft(samples, axis=0)
    return jnp.stack([jnp.real(spectra), jnp.imag(spectra)]).astype(jnp.bfloat16)

def reference(cube, train_blocks, guard_blocks, prior_factor, steering):
    spectrum = lax.map(one_channel, jnp.moveaxis(cube, 1, 0))
    usable = jnp.repeat(train_blocks * guard_blocks[None, :], BLOCK, axis=1).astype(jnp.bfloat16)
    half = NDOF // 2

    def one_bin(index):
        after = ((index + 1) % P_SIZE).astype(jnp.int32)
        current = lax.dynamic_index_in_dim(spectrum, index, axis=2, keepdims=False)
        following = lax.dynamic_index_in_dim(spectrum, after, axis=2, keepdims=False)
        vectors = jnp.concatenate([current[:, 0], following[:, 0], current[:, 1], following[:, 1]], axis=0)
        gate_mask = lax.dynamic_index_in_dim(usable, index, axis=0, keepdims=False)
        masked = vectors * gate_mask[None, :]
        gram = jnp.dot(masked.astype(jnp.float32), masked.T.astype(jnp.float32), preferred_element_type=jnp.float32)
        real_part = gram[:half, :half] + gram[half:, half:]
        cross = gram[half:, :half] - gram[:half, half:]
        top = jnp.concatenate([real_part, -cross], axis=1)
        bottom = jnp.concatenate([cross, real_part], axis=1)
        prior_k = lax.dynamic_index_in_dim(prior_factor, index, axis=0, keepdims=False)
        prior_gram = jnp.dot(prior_k.T, prior_k, precision=lax.Precision.HIGHEST)
        covariance = jnp.concatenate([top, bottom], axis=0) + 0.98 * prior_gram
        lower = jnp.linalg.cholesky(covariance)
        target = lax.dynamic_index_in_dim(steering, index, axis=0, keepdims=False)[:, None]
        first = lax.linalg.triangular_solve(lower, target, left_side=True, lower=True)
        second = lax.linalg.triangular_solve(lower, first, left_side=True, lower=True, transpose_a=True)
        weight = second[:, 0] / jnp.sum(first * first)
        rotated = jnp.concatenate([-weight[half:], weight[:half]])
        stacked = jnp.stack([weight, rotated]).astype(jnp.bfloat16)
        output = jnp.dot(stacked.astype(jnp.float32), vectors.astype(jnp.float32), preferred_element_type=jnp.float32)
        return (output, lower.T)
    outputs, factors = lax.map(one_bin, jnp.arange(P_SIZE, dtype=jnp.int32))
    return (jnp.moveaxis(outputs, 1, 0), factors)
```

```python
import math

import jax
import jax.numpy as jnp
from jax import lax
from jax.experimental import pallas as pl
from jax.experimental.pallas import tpu as pltpu
from jax.sharding import PartitionSpec as P

BLOCK = 128
BINS = 8
LANES = 128
PANEL = 8

forgetting = 0.98


def from_behind(block, axis, distance):
    devices = range(lax.axis_size(axis))
    route = [((i - distance) % len(devices), i) for i in devices]
    return lax.ppermute(block, axis, route)


def dft_table(pulses):
    index = jnp.arange(pulses, dtype=jnp.int32)
    product = index[:, None] * index[None, :] % pulses
    angle = product.astype(jnp.float32) * (2.0 * math.pi / pulses)
    cosine = jnp.cos(angle)
    sine = jnp.sin(angle)
    top = jnp.stack([cosine, -sine], axis=1)
    bottom = jnp.stack([sine, cosine], axis=1)
    return jnp.stack([top, bottom], axis=0)


def spectra(pulse_block, table):
    out = jnp.einsum(
        "scpg,sptk->tckg", pulse_block.astype(jnp.float32), table, precision=lax.Precision.HIGHEST
    )
    return out.astype(jnp.bfloat16)


def lane(x, index):
    where = jnp.full((BINS, LANES), index, jnp.int32)
    return jnp.take_along_axis(x, where, axis=1, mode="promise_in_bounds")


def factor_kernel(cov_ref, steer_ref, out_ref, weight_ref, left, right):
    halves = (left, right)
    at = lax.broadcasted_iota(jnp.int32, (BINS, LANES), 1)
    for h in range(2):
        halves[h][...] = cov_ref[:, h * LANES : (h + 1) * LANES]

    def rows(j):
        return pl.ds(pl.multiple_of(j * BINS, BINS), BINS)

    def panel(h, p, carry):
        s, q, vv = carry
        o = p * PANEL
        base = h * LANES + o
        pair = [[halves[c][rows(base + i), :] for c in range(2)] for i in range(PANEL)]
        final = []
        for j in range(PANEL):
            own = at == o + j
            pivot = lane(pair[j][h], o + j)
            inv = lax.rsqrt(pivot)
            inv2 = inv * inv
            source = list(pair[j])
            source[h] = jnp.where(own, 1.0, source[h])
            for i in range(j + 1, PANEL):
                m = lane(pair[j][h], o + i) * inv2
                target = list(pair[i])
                target[h] = jnp.where(own, 0.0, target[h])
                pair[i] = [target[c] - m * source[c] for c in range(2)]
            row = [source[c] * inv for c in range(2)]
            v = lane(s[h], o + j) * inv
            s = [s[c] - v * row[c] for c in range(2)]
            below = [row[0], jnp.zeros_like(row[1])] if h else [row[0], jnp.zeros_like(row[1])]
            below[h] = jnp.where(at <= o + j, row[h], 0.0)
            q = [q[c] + v * below[c] for c in range(2)]
            vv = vv + v * v
            shown = list(row)
            if h:
                shown[0] = jnp.zeros_like(row[0])
            shown[h] = jnp.where(own, pivot * inv, jnp.where(at > o + j, row[h], 0.0))
            for c in range(2):
                halves[c][rows(base + j), :] = row[c]
                out_ref[rows(base + j), c * LANES : (c + 1) * LANES] = shown[c]
            row[h] = jnp.where((at > o + j) & (at < o + PANEL), 0.0, row[h])
            final.append(row)
        inside = (at >= o) & (at < o + PANEL)

        def group(g, _):
            for i in range(PANEL):
                index = g * PANEL + i
                place = rows(h * LANES + index)
                target = [halves[c][place, :] for c in range(2)]
                target[h] = jnp.where(inside, 0.0, target[h])
                for k in range(PANEL):
                    m = lane(final[k][h], index)
                    target = [target[c] - m * final[k][c] for c in range(2)]
                for c in range(2):
                    halves[c][place, :] = target[c]
            return 0

        lax.fori_loop(p + 1, LANES // PANEL, group, 0)
        return s, q, vv

    zero = jnp.zeros((BINS, LANES), jnp.float32)
    s = [steer_ref[:, c * LANES : (c + 1) * LANES] for c in range(2)]
    carry = (s, [zero, zero], zero)
    carry = lax.fori_loop(0, LANES // PANEL, lambda p, c: panel(0, p, c), carry)

    row_id = lax.broadcasted_iota(jnp.int32, (LANES, LANES), 0)
    col_id = lax.broadcasted_iota(jnp.int32, (LANES, LANES), 1)
    for b in range(BINS):
        top = pl.ds(b, LANES, stride=BINS)
        bottom = pl.ds(LANES * BINS + b, LANES, stride=BINS)
        upper = right[top, :]
        inverse = jnp.where(col_id <= row_id, left[top, :], 0.0)
        across = upper.T
        left[bottom, :] = -jnp.dot(
            across, inverse, precision=lax.Precision.HIGHEST, preferred_element_type=jnp.float32
        )
        right[bottom, :] = right[bottom, :] - jnp.dot(
            across, upper, precision=lax.Precision.HIGHEST, preferred_element_type=jnp.float32
        )

    s, q, vv = lax.fori_loop(0, LANES // PANEL, lambda p, c: panel(1, p, c), carry)
    for c in range(2):
        weight_ref[:, c * LANES : (c + 1) * LANES] = q[c] / vv


def factorize(covariance, steering):
    n = covariance.shape[0]
    flat = covariance.reshape(n * BINS, n)
    factor, weight = pl.pallas_call(
        factor_kernel,
        out_shape=(
            jax.ShapeDtypeStruct((n * BINS, n), jnp.float32),
            jax.ShapeDtypeStruct((BINS, n), jnp.float32),
        ),
        in_specs=[pl.BlockSpec(memory_space=pltpu.VMEM)] * 2,
        out_specs=(pl.BlockSpec(memory_space=pltpu.VMEM), pl.BlockSpec(memory_space=pltpu.VMEM)),
        scratch_shapes=[pltpu.VMEM((n * BINS, LANES), jnp.float32)] * 2,
        compiler_params=pltpu.CompilerParams(vmem_limit_bytes=40 * 1024 * 1024),
    )(flat, steering)
    return factor.reshape(n, BINS, n), weight


def shards(cube, train_blocks, guard_blocks, prior_factor, steering):
    rows = prior_factor.shape[1]
    prior = lax.all_gather(prior_factor, "rng", axis=1, tiled=True)
    prior_gram = forgetting * jnp.einsum(
        "krd,kre->kde", prior, prior, precision=lax.Precision.HIGHEST
    )
    table = dft_table(cube.shape[2] * lax.axis_size("dop"))
    pulse_block = lax.all_to_all(cube, "dop", split_axis=3, concat_axis=2, tiled=True)
    spectrum = lax.all_to_all(
        spectra(pulse_block, table), "dop", split_axis=2, concat_axis=3, tiled=True
    )
    neighbor = from_behind(spectrum[:, :, 0:1, :], "dop", -1)
    following = jnp.concatenate([spectrum[:, :, 1:, :], neighbor], axis=2)
    vectors = jnp.concatenate([spectrum[0], following[0], spectrum[1], following[1]], axis=0)
    usable = train_blocks * guard_blocks[None, :]
    gate_mask = jnp.repeat(usable, BLOCK, axis=1).astype(jnp.bfloat16)
    masked = vectors * gate_mask[None, :, :]
    half = vectors.shape[0] // 2
    gram = jnp.einsum("dkg,ekg->kde", masked, masked, preferred_element_type=jnp.float32)
    real_part = gram[:, :half, :half] + gram[:, half:, half:]
    cross = gram[:, half:, :half] - gram[:, :half, half:]
    row_id = lax.broadcasted_iota(jnp.int32, (1, half, half), 1)
    col_id = lax.broadcasted_iota(jnp.int32, (1, half, half), 2)
    packed = lax.psum(jnp.where(row_id <= col_id, real_part, cross), "rng")
    flipped = jnp.swapaxes(packed, 1, 2)
    real_part = jnp.where(row_id <= col_id, packed, flipped)
    cross = jnp.where(row_id > col_id, packed, jnp.where(row_id < col_id, -flipped, 0.0))
    top = jnp.concatenate([real_part, -cross], axis=2)
    bottom = jnp.concatenate([cross, real_part], axis=2)
    covariance = jnp.concatenate([top, bottom], axis=1) + prior_gram
    upper, weight = factorize(jnp.swapaxes(covariance, 0, 1), steering)
    rotated = jnp.concatenate([-weight[:, half:], weight[:, :half]], axis=1)
    stacked = jnp.stack([weight, rotated]).astype(jnp.bfloat16)
    filtered = jnp.einsum("skd,dkg->skg", stacked, vectors, preferred_element_type=jnp.float32)
    start = lax.axis_index("rng") * rows
    factor = jnp.swapaxes(lax.dynamic_slice_in_dim(upper, start, rows, axis=0), 0, 1)
    return (filtered, factor)


def solution(mesh):
    return jax.shard_map(
        shards,
        mesh=mesh,
        in_specs=(
            P(None, None, "dop", "rng"),
            P("dop", "rng"),
            P("rng"),
            P("dop", "rng", None),
            P("dop", None),
        ),
        out_specs=(P(None, "dop", "rng"), P("dop", "rng", None)),
        check_vma=False,
    )
```

```python
import functools
import math

import jax
import jax.numpy as jnp
from jax import lax
from jax.experimental import pallas as pl
from jax.experimental.pallas import tpu as pltpu
from jax.sharding import PartitionSpec as P

BLOCK = 128
BINS = 8
LANES = 128
PANEL = 8

forgetting = 0.98


def from_behind(block, axis, distance):
    devices = range(lax.axis_size(axis))
    route = [((i - distance) % len(devices), i) for i in devices]
    return lax.ppermute(block, axis, route)


def dft_table(pulses):
    index = jnp.arange(pulses, dtype=jnp.int32)
    product = index[:, None] * index[None, :] % pulses
    angle = product.astype(jnp.float32) * (2.0 * math.pi / pulses)
    cosine = jnp.cos(angle)
    sine = jnp.sin(angle)
    top = jnp.stack([cosine, -sine], axis=1)
    bottom = jnp.stack([sine, cosine], axis=1)
    return jnp.stack([top, bottom], axis=0)


def spectra(pulse_block, table):
    out = jnp.einsum(
        "scpg,sptk->tckg", pulse_block.astype(jnp.float32), table, precision=lax.Precision.HIGHEST
    )
    return out.astype(jnp.bfloat16)


def lane(x, index):
    where = jnp.full((BINS, LANES), index, jnp.int32)
    return jnp.take_along_axis(x, where, axis=1, mode="promise_in_bounds")


def factor_kernel(cov_ref, steer_ref, out_ref, weight_ref, left, right):
    halves = (left, right)
    at = lax.broadcasted_iota(jnp.int32, (BINS, LANES), 1)
    for h in range(2):
        halves[h][...] = cov_ref[:, h * LANES : (h + 1) * LANES]

    def rows(j):
        return pl.ds(pl.multiple_of(j * BINS, BINS), BINS)

    def panel(h, p, carry):
        s, q, vv = carry
        o = p * PANEL
        base = h * LANES + o
        pair = [[halves[c][rows(base + i), :] for c in range(2)] for i in range(PANEL)]
        final = []
        for j in range(PANEL):
            own = at == o + j
            pivot = lane(pair[j][h], o + j)
            inv = lax.rsqrt(pivot)
            inv2 = inv * inv
            source = list(pair[j])
            source[h] = jnp.where(own, 1.0, source[h])
            for i in range(j + 1, PANEL):
                m = lane(pair[j][h], o + i) * inv2
                target = list(pair[i])
                target[h] = jnp.where(own, 0.0, target[h])
                pair[i] = [target[c] - m * source[c] for c in range(2)]
            row = [source[c] * inv for c in range(2)]
            v = lane(s[h], o + j) * inv
            s = [s[c] - v * row[c] for c in range(2)]
            below = [row[0], jnp.zeros_like(row[1])] if h else [row[0], jnp.zeros_like(row[1])]
            below[h] = jnp.where(at <= o + j, row[h], 0.0)
            q = [q[c] + v * below[c] for c in range(2)]
            vv = vv + v * v
            shown = list(row)
            if h:
                shown[0] = jnp.zeros_like(row[0])
            shown[h] = jnp.where(own, pivot * inv, jnp.where(at > o + j, row[h], 0.0))
            for c in range(2):
                halves[c][rows(base + j), :] = row[c]
                out_ref[rows(base + j), c * LANES : (c + 1) * LANES] = shown[c]
            row[h] = jnp.where((at > o + j) & (at < o + PANEL), 0.0, row[h])
            final.append(row)
        inside = (at >= o) & (at < o + PANEL)

        def group(g, _):
            for i in range(PANEL):
                index = g * PANEL + i
                place = rows(h * LANES + index)
                target = [halves[c][place, :] for c in range(2)]
                target[h] = jnp.where(inside, 0.0, target[h])
                for k in range(PANEL):
                    m = lane(final[k][h], index)
                    target = [target[c] - m * final[k][c] for c in range(2)]
                for c in range(2):
                    halves[c][place, :] = target[c]
            return 0

        lax.fori_loop(p + 1, LANES // PANEL, group, 0)
        return s, q, vv

    zero = jnp.zeros((BINS, LANES), jnp.float32)
    s = [steer_ref[:, c * LANES : (c + 1) * LANES] for c in range(2)]
    carry = (s, [zero, zero], zero)
    carry = lax.fori_loop(0, LANES // PANEL, lambda p, c: panel(0, p, c), carry)

    row_id = lax.broadcasted_iota(jnp.int32, (LANES, LANES), 0)
    col_id = lax.broadcasted_iota(jnp.int32, (LANES, LANES), 1)
    for b in range(BINS):
        top = pl.ds(b, LANES, stride=BINS)
        bottom = pl.ds(LANES * BINS + b, LANES, stride=BINS)
        upper = right[top, :]
        inverse = jnp.where(col_id <= row_id, left[top, :], 0.0)
        across = upper.T
        left[bottom, :] = -jnp.dot(
            across, inverse, precision=lax.Precision.HIGHEST, preferred_element_type=jnp.float32
        )
        right[bottom, :] = right[bottom, :] - jnp.dot(
            across, upper, precision=lax.Precision.HIGHEST, preferred_element_type=jnp.float32
        )

    s, q, vv = lax.fori_loop(0, LANES // PANEL, lambda p, c: panel(1, p, c), carry)
    for c in range(2):
        weight_ref[:, c * LANES : (c + 1) * LANES] = q[c] / vv


def sum_kernel(n, part_ref, out_ref, slots, send1, recv1, send2, recv2):
    me = lax.axis_index("rng")
    row = lax.axis_index("dop")

    def other(d):
        return lax.rem(me + d, n)

    def source(d):
        return lax.rem(me + n - d, n)

    barrier = pltpu.get_barrier_semaphore()

    def greet(d, _):
        pl.semaphore_signal(
            barrier, inc=1, device_id=(row, other(d)), device_id_type=pl.DeviceIdType.MESH
        )
        return 0

    lax.fori_loop(1, n, greet, 0)
    pl.semaphore_wait(barrier, n - 1)

    def scatter(d):
        return pltpu.make_async_remote_copy(
            src_ref=part_ref.at[other(d)],
            dst_ref=slots.at[d],
            send_sem=send1.at[d],
            recv_sem=recv1.at[d],
            device_id=(row, other(d)),
            device_id_type=pl.DeviceIdType.MESH,
        )

    def spread(d, chunk):
        return pltpu.make_async_remote_copy(
            src_ref=out_ref.at[chunk],
            dst_ref=out_ref.at[chunk],
            send_sem=send2.at[d],
            recv_sem=recv2.at[d],
            device_id=(row, other(d)),
            device_id_type=pl.DeviceIdType.MESH,
        )

    def start_scatter(d, _):
        scatter(d).start()
        return 0

    lax.fori_loop(1, n, start_scatter, 0)

    def add(d, total):
        scatter(d).wait_recv()
        return total + slots[d]

    out_ref[me] = lax.fori_loop(1, n, add, part_ref[me])

    def start_spread(d, _):
        spread(d, me).start()
        return 0

    lax.fori_loop(1, n, start_spread, 0)

    def finish(d, _):
        scatter(d).wait_send()
        spread(d, me).wait_send()
        spread(d, source(d)).wait_recv()
        return 0

    lax.fori_loop(1, n, finish, 0)


def sum_over_rng(part):
    n = lax.axis_size("rng")
    chunks = part.reshape(n, -1, LANES)
    size = chunks.shape[1]
    total = pl.pallas_call(
        functools.partial(sum_kernel, n),
        out_shape=jax.ShapeDtypeStruct(chunks.shape, jnp.float32),
        in_specs=[pl.BlockSpec(memory_space=pltpu.VMEM)],
        out_specs=pl.BlockSpec(memory_space=pltpu.VMEM),
        scratch_shapes=[pltpu.VMEM((n, size, LANES), jnp.float32)]
        + [pltpu.SemaphoreType.DMA((n,))] * 4,
        compiler_params=pltpu.CompilerParams(collective_id=0, has_side_effects=True),
    )(chunks)
    return total.reshape(part.shape)


def factorize(covariance, steering):
    n = covariance.shape[0]
    flat = covariance.reshape(n * BINS, n)
    factor, weight = pl.pallas_call(
        factor_kernel,
        out_shape=(
            jax.ShapeDtypeStruct((n * BINS, n), jnp.float32),
            jax.ShapeDtypeStruct((BINS, n), jnp.float32),
        ),
        in_specs=[pl.BlockSpec(memory_space=pltpu.VMEM)] * 2,
        out_specs=(pl.BlockSpec(memory_space=pltpu.VMEM), pl.BlockSpec(memory_space=pltpu.VMEM)),
        scratch_shapes=[pltpu.VMEM((n * BINS, LANES), jnp.float32)] * 2,
        compiler_params=pltpu.CompilerParams(vmem_limit_bytes=40 * 1024 * 1024),
    )(flat, steering)
    return factor.reshape(n, BINS, n), weight


def shards(cube, train_blocks, guard_blocks, prior_factor, steering):
    rows = prior_factor.shape[1]
    prior = lax.all_gather(prior_factor, "rng", axis=1, tiled=True)
    table = dft_table(cube.shape[2] * lax.axis_size("dop"))
    pulse_block = lax.all_to_all(cube, "dop", split_axis=3, concat_axis=2, tiled=True)
    spectrum = lax.all_to_all(
        spectra(pulse_block, table), "dop", split_axis=2, concat_axis=3, tiled=True
    )
    spectrum, prior = lax.optimization_barrier((spectrum, prior))
    neighbor = from_behind(spectrum[:, :, 0:1, :], "dop", -1)
    following = jnp.concatenate([spectrum[:, :, 1:, :], neighbor], axis=2)
    vectors = jnp.concatenate([spectrum[0], following[0], spectrum[1], following[1]], axis=0)
    usable = train_blocks * guard_blocks[None, :]
    gate_mask = jnp.repeat(usable, BLOCK, axis=1).astype(jnp.bfloat16)
    masked = vectors * gate_mask[None, :, :]
    half = vectors.shape[0] // 2
    gram = jnp.einsum("dkg,ekg->kde", masked, masked, preferred_element_type=jnp.float32)
    real_part = gram[:, :half, :half] + gram[:, half:, half:]
    cross = gram[:, half:, :half] - gram[:, :half, half:]
    row_id = lax.broadcasted_iota(jnp.int32, (1, half, half), 1)
    col_id = lax.broadcasted_iota(jnp.int32, (1, half, half), 2)
    prior_gram = forgetting * jnp.einsum(
        "krd,kre->kde", prior, prior, precision=lax.Precision.HIGHEST
    )
    packed = sum_over_rng(jnp.where(row_id <= col_id, real_part, cross))
    flipped = jnp.swapaxes(packed, 1, 2)
    real_part = jnp.where(row_id <= col_id, packed, flipped)
    cross = jnp.where(row_id > col_id, packed, jnp.where(row_id < col_id, -flipped, 0.0))
    top = jnp.concatenate([real_part, -cross], axis=2)
    bottom = jnp.concatenate([cross, real_part], axis=2)
    covariance = jnp.concatenate([top, bottom], axis=1) + prior_gram
    upper, weight = factorize(jnp.swapaxes(covariance, 0, 1), steering)
    rotated = jnp.concatenate([-weight[:, half:], weight[:, :half]], axis=1)
    stacked = jnp.stack([weight, rotated]).astype(jnp.bfloat16)
    filtered = jnp.einsum("skd,dkg->skg", stacked, vectors, preferred_element_type=jnp.float32)
    start = lax.axis_index("rng") * rows
    factor = jnp.swapaxes(lax.dynamic_slice_in_dim(upper, start, rows, axis=0), 0, 1)
    return (filtered, factor)


def solution(mesh):
    return jax.shard_map(
        shards,
        mesh=mesh,
        in_specs=(
            P(None, None, "dop", "rng"),
            P("dop", "rng"),
            P("rng"),
            P("dop", "rng", None),
            P("dop", None),
        ),
        out_specs=(P(None, "dop", "rng"), P("dop", "rng", None)),
        check_vma=False,
    )
```

```python
import functools
import math

import jax
import jax.numpy as jnp
from jax import lax
from jax.experimental import pallas as pl
from jax.experimental.pallas import tpu as pltpu
from jax.sharding import PartitionSpec as P

BLOCK = 128
BINS = 8
LANES = 128
PANEL = 8
COLUMN = 8

forgetting = 0.98


def from_behind(block, axis, distance):
    devices = range(lax.axis_size(axis))
    route = [((i - distance) % len(devices), i) for i in devices]
    return lax.ppermute(block, axis, route)


def dft_table(pulses):
    index = jnp.arange(pulses, dtype=jnp.int32)
    product = index[:, None] * index[None, :] % pulses
    angle = product.astype(jnp.float32) * (2.0 * math.pi / pulses)
    cosine = jnp.cos(angle)
    sine = jnp.sin(angle)
    top = jnp.stack([cosine, -sine], axis=1)
    bottom = jnp.stack([sine, cosine], axis=1)
    return jnp.stack([top, bottom], axis=0)


def spectra(pulse_block, table):
    out = jnp.einsum(
        "scpg,sptk->tckg", pulse_block.astype(jnp.float32), table, precision=lax.Precision.HIGHEST
    )
    return out.astype(jnp.bfloat16)


def lane(x, index):
    where = jnp.full((BINS, LANES), index, jnp.int32)
    return jnp.take_along_axis(x, where, axis=1, mode="promise_in_bounds")


def factor_kernel(cov_ref, steer_ref, out_ref, weight_ref, left, right):
    halves = (left, right)
    at = lax.broadcasted_iota(jnp.int32, (BINS, LANES), 1)
    for h in range(2):
        halves[h][...] = cov_ref[:, h * LANES : (h + 1) * LANES]

    def rows(j):
        return pl.ds(pl.multiple_of(j * BINS, BINS), BINS)

    def panel(h, p, carry):
        s, q, vv = carry
        o = p * PANEL
        base = h * LANES + o
        pair = [[halves[c][rows(base + i), :] for c in range(2)] for i in range(PANEL)]
        block = [[lane(pair[j][h], o + i) if i >= j else None for i in range(PANEL)] for j in range(PANEL)]
        side = [lane(s[h], o + j) for j in range(PANEL)]
        final = []
        for j in range(PANEL):
            own = at == o + j
            pivot = block[j][j]
            inv = lax.rsqrt(pivot)
            inv2 = inv * inv
            ratio = [block[j][i] * inv2 if i > j else None for i in range(PANEL)]
            for i in range(j + 1, PANEL):
                for l in range(i, PANEL):
                    block[i][l] = block[i][l] - ratio[i] * block[j][l]
                side[i] = side[i] - ratio[i] * side[j]
            source = list(pair[j])
            source[h] = jnp.where(own, 1.0, source[h])
            for i in range(j + 1, PANEL):
                target = list(pair[i])
                target[h] = jnp.where(own, 0.0, target[h])
                pair[i] = [target[c] - ratio[i] * source[c] for c in range(2)]
            row = [source[c] * inv for c in range(2)]
            v = side[j] * inv
            s = [s[c] - v * row[c] for c in range(2)]
            below = [row[0], jnp.zeros_like(row[1])]
            below[h] = jnp.where(at <= o + j, row[h], 0.0)
            q = [q[c] + v * below[c] for c in range(2)]
            vv = vv + v * v
            shown = list(row)
            if h:
                shown[0] = jnp.zeros_like(row[0])
            shown[h] = jnp.where(own, pivot * inv, jnp.where(at > o + j, row[h], 0.0))
            for c in range(2):
                halves[c][rows(base + j), :] = row[c]
                out_ref[rows(base + j), c * LANES : (c + 1) * LANES] = shown[c]
            row[h] = jnp.where((at > o + j) & (at < o + PANEL), 0.0, row[h])
            final.append(row)
        inside = (at >= o) & (at < o + PANEL)

        def group(g, _):
            for i in range(PANEL):
                index = g * PANEL + i
                place = rows(h * LANES + index)
                target = [halves[c][place, :] for c in range(2)]
                target[h] = jnp.where(inside, 0.0, target[h])
                for k in range(PANEL):
                    m = lane(final[k][h], index)
                    target = [target[c] - m * final[k][c] for c in range(2)]
                for c in range(2):
                    halves[c][place, :] = target[c]
            return 0

        lax.fori_loop(p + 1, LANES // PANEL, group, 0)
        return s, q, vv

    zero = jnp.zeros((BINS, LANES), jnp.float32)
    s = [steer_ref[:, c * LANES : (c + 1) * LANES] for c in range(2)]
    carry = (s, [zero, zero], zero)
    carry = lax.fori_loop(0, LANES // PANEL, lambda p, c: panel(0, p, c), carry)

    row_id = lax.broadcasted_iota(jnp.int32, (LANES, LANES), 0)
    col_id = lax.broadcasted_iota(jnp.int32, (LANES, LANES), 1)
    for b in range(BINS):
        top = pl.ds(b, LANES, stride=BINS)
        bottom = pl.ds(LANES * BINS + b, LANES, stride=BINS)
        upper = right[top, :]
        inverse = jnp.where(col_id <= row_id, left[top, :], 0.0)
        across = upper.T
        left[bottom, :] = -jnp.dot(
            across, inverse, precision=lax.Precision.HIGHEST, preferred_element_type=jnp.float32
        )
        right[bottom, :] = right[bottom, :] - jnp.dot(
            across, upper, precision=lax.Precision.HIGHEST, preferred_element_type=jnp.float32
        )

    s, q, vv = lax.fori_loop(0, LANES // PANEL, lambda p, c: panel(1, p, c), carry)
    for c in range(2):
        weight_ref[:, c * LANES : (c + 1) * LANES] = q[c] / vv


def sum_kernel(nx, ny, part_ref, out_ref, slots_x, held, slots_y, sends, arrivals):
    me = lax.axis_index("rng")
    row = lax.axis_index("dop")
    x = me // ny
    y = lax.rem(me, ny)

    def along_x(d):
        return (row, lax.rem(x + d, nx) * ny + y)

    def along_y(d):
        return (row, x * ny + lax.rem(y + d, ny))

    barrier = pltpu.get_barrier_semaphore()
    for d in range(1, nx):
        pl.semaphore_signal(
            barrier, inc=1, device_id=along_x(d), device_id_type=pl.DeviceIdType.MESH
        )
    for d in range(1, ny):
        pl.semaphore_signal(
            barrier, inc=1, device_id=along_y(d), device_id_type=pl.DeviceIdType.MESH
        )
    pl.semaphore_wait(barrier, nx + ny - 2)

    def copy(source, target, stage, d, device):
        return pltpu.make_async_remote_copy(
            src_ref=source,
            dst_ref=target,
            send_sem=sends.at[stage, d],
            recv_sem=arrivals.at[stage, d],
            device_id=device,
            device_id_type=pl.DeviceIdType.MESH,
        )

    def scatter_x(d):
        return copy(part_ref.at[lax.rem(x + d, nx)], slots_x.at[d], 0, d, along_x(d))

    def scatter_y(d):
        return copy(held.at[lax.rem(y + d, ny)], slots_y.at[d], 1, d, along_y(d))

    def gather_y(d, place):
        return copy(out_ref.at[x, place], out_ref.at[x, place], 2, d, along_y(d))

    def gather_x(d, place):
        return copy(out_ref.at[place], out_ref.at[place], 3, d, along_x(d))

    for d in range(1, nx):
        scatter_x(d).start()
    for d in range(1, nx):
        scatter_x(d).wait_recv()
    total = part_ref[x]
    for d in range(1, nx):
        total = total + slots_x[d]
    held[...] = total
    for d in range(1, ny):
        scatter_y(d).start()
    for d in range(1, ny):
        scatter_y(d).wait_recv()
    total = held[y]
    for d in range(1, ny):
        total = total + slots_y[d]
    out_ref[x, y] = total
    for d in range(1, ny):
        gather_y(d, y).start()
    for d in range(1, ny):
        gather_y(d, lax.rem(y + ny - d, ny)).wait_recv()
    for d in range(1, nx):
        gather_x(d, x).start()
    for d in range(1, nx):
        gather_x(d, lax.rem(x + nx - d, nx)).wait_recv()
    for d in range(1, nx):
        scatter_x(d).wait_send()
        gather_x(d, x).wait_send()
    for d in range(1, ny):
        scatter_y(d).wait_send()
        gather_y(d, y).wait_send()


def sum_over_rng(part):
    n = lax.axis_size("rng")
    ny = COLUMN
    nx = n // ny
    chunks = part.reshape(nx, ny, -1, LANES)
    size = chunks.shape[2]
    total = pl.pallas_call(
        functools.partial(sum_kernel, nx, ny),
        out_shape=jax.ShapeDtypeStruct(chunks.shape, jnp.float32),
        in_specs=[pl.BlockSpec(memory_space=pltpu.VMEM)],
        out_specs=pl.BlockSpec(memory_space=pltpu.VMEM),
        scratch_shapes=[
            pltpu.VMEM((nx, ny, size, LANES), jnp.float32),
            pltpu.VMEM((ny, size, LANES), jnp.float32),
            pltpu.VMEM((ny, size, LANES), jnp.float32),
            pltpu.SemaphoreType.DMA((4, ny)),
            pltpu.SemaphoreType.DMA((4, ny)),
        ],
        compiler_params=pltpu.CompilerParams(collective_id=0, has_side_effects=True),
    )(chunks)
    return total.reshape(part.shape)


def factorize(covariance, steering):
    n = covariance.shape[0]
    flat = covariance.reshape(n * BINS, n)
    factor, weight = pl.pallas_call(
        factor_kernel,
        out_shape=(
            jax.ShapeDtypeStruct((n * BINS, n), jnp.float32),
            jax.ShapeDtypeStruct((BINS, n), jnp.float32),
        ),
        in_specs=[pl.BlockSpec(memory_space=pltpu.VMEM)] * 2,
        out_specs=(pl.BlockSpec(memory_space=pltpu.VMEM), pl.BlockSpec(memory_space=pltpu.VMEM)),
        scratch_shapes=[pltpu.VMEM((n * BINS, LANES), jnp.float32)] * 2,
        compiler_params=pltpu.CompilerParams(vmem_limit_bytes=40 * 1024 * 1024),
    )(flat, steering)
    return factor.reshape(n, BINS, n), weight


def shards(cube, train_blocks, guard_blocks, prior_factor, steering):
    rows = prior_factor.shape[1]
    prior = lax.all_gather(prior_factor, "rng", axis=1, tiled=True)
    table = dft_table(cube.shape[2] * lax.axis_size("dop"))
    pulse_block = lax.all_to_all(cube, "dop", split_axis=3, concat_axis=2, tiled=True)
    spectrum = lax.all_to_all(
        spectra(pulse_block, table), "dop", split_axis=2, concat_axis=3, tiled=True
    )
    spectrum, prior = lax.optimization_barrier((spectrum, prior))
    neighbor = from_behind(spectrum[:, :, 0:1, :], "dop", -1)
    following = jnp.concatenate([spectrum[:, :, 1:, :], neighbor], axis=2)
    vectors = jnp.concatenate([spectrum[0], following[0], spectrum[1], following[1]], axis=0)
    usable = train_blocks * guard_blocks[None, :]
    gate_mask = jnp.repeat(usable, BLOCK, axis=1).astype(jnp.bfloat16)
    masked = vectors * gate_mask[None, :, :]
    half = vectors.shape[0] // 2
    gram = jnp.einsum("dkg,ekg->kde", masked, masked, preferred_element_type=jnp.float32)
    real_part = gram[:, :half, :half] + gram[:, half:, half:]
    cross = gram[:, half:, :half] - gram[:, :half, half:]
    row_id = lax.broadcasted_iota(jnp.int32, (1, half, half), 1)
    col_id = lax.broadcasted_iota(jnp.int32, (1, half, half), 2)
    prior_gram = forgetting * jnp.einsum(
        "krd,kre->kde", prior, prior, precision=lax.Precision.HIGHEST
    )
    packed = sum_over_rng(jnp.where(row_id <= col_id, real_part, cross))
    flipped = jnp.swapaxes(packed, 1, 2)
    real_part = jnp.where(row_id <= col_id, packed, flipped)
    cross = jnp.where(row_id > col_id, packed, jnp.where(row_id < col_id, -flipped, 0.0))
    top = jnp.concatenate([real_part, -cross], axis=2)
    bottom = jnp.concatenate([cross, real_part], axis=2)
    covariance = jnp.concatenate([top, bottom], axis=1) + prior_gram
    upper, weight = factorize(jnp.swapaxes(covariance, 0, 1), steering)
    rotated = jnp.concatenate([-weight[:, half:], weight[:, :half]], axis=1)
    stacked = jnp.stack([weight, rotated]).astype(jnp.bfloat16)
    filtered = jnp.einsum("skd,dkg->skg", stacked, vectors, preferred_element_type=jnp.float32)
    start = lax.axis_index("rng") * rows
    factor = jnp.swapaxes(lax.dynamic_slice_in_dim(upper, start, rows, axis=0), 0, 1)
    return (filtered, factor)


def solution(mesh):
    return jax.shard_map(
        shards,
        mesh=mesh,
        in_specs=(
            P(None, None, "dop", "rng"),
            P("dop", "rng"),
            P("rng"),
            P("dop", "rng", None),
            P("dop", None),
        ),
        out_specs=(P(None, "dop", "rng"), P("dop", "rng", None)),
        check_vma=False,
    )
```

```python
import functools
import math

import jax
import jax.numpy as jnp
from jax import lax
from jax.experimental import pallas as pl
from jax.experimental.pallas import tpu as pltpu
from jax.sharding import PartitionSpec as P

BLOCK = 128
BINS = 8
LANES = 128
PANEL = 8
COLUMN = 8

forgetting = 0.98


def from_behind(block, axis, distance):
    devices = range(lax.axis_size(axis))
    route = [((i - distance) % len(devices), i) for i in devices]
    return lax.ppermute(block, axis, route)


def dft_table(pulses):
    index = jnp.arange(pulses, dtype=jnp.int32)
    product = index[:, None] * index[None, :] % pulses
    angle = product.astype(jnp.float32) * (2.0 * math.pi / pulses)
    cosine = jnp.cos(angle)
    sine = jnp.sin(angle)
    top = jnp.stack([cosine, -sine], axis=1)
    bottom = jnp.stack([sine, cosine], axis=1)
    return jnp.stack([top, bottom], axis=0)


def spectra(pulse_block, table):
    out = jnp.einsum(
        "scpg,sptk->tckg", pulse_block.astype(jnp.float32), table, precision=lax.Precision.HIGHEST
    )
    return out.astype(jnp.bfloat16)


def lane(x, index):
    where = jnp.full((BINS, LANES), index, jnp.int32)
    return jnp.take_along_axis(x, where, axis=1, mode="promise_in_bounds")


def factor_kernel(cov_ref, steer_ref, out_ref, weight_ref, left, right):
    halves = (left, right)
    at = lax.broadcasted_iota(jnp.int32, (BINS, LANES), 1)
    for h in range(2):
        halves[h][...] = cov_ref[:, h * LANES : (h + 1) * LANES]

    def rows(j):
        return pl.ds(pl.multiple_of(j * BINS, BINS), BINS)

    def panel(h, p, carry):
        s, q, vv = carry
        o = p * PANEL
        base = h * LANES + o
        pair = [[halves[c][rows(base + i), :] for c in range(2)] for i in range(PANEL)]
        block = [[lane(pair[j][h], o + i) if i >= j else None for i in range(PANEL)] for j in range(PANEL)]
        side = [lane(s[h], o + j) for j in range(PANEL)]
        final = []
        for j in range(PANEL):
            own = at == o + j
            pivot = block[j][j]
            inv = lax.rsqrt(pivot)
            inv2 = inv * inv
            ratio = [block[j][i] * inv2 if i > j else None for i in range(PANEL)]
            for i in range(j + 1, PANEL):
                for l in range(i, PANEL):
                    block[i][l] = block[i][l] - ratio[i] * block[j][l]
                side[i] = side[i] - ratio[i] * side[j]
            source = list(pair[j])
            source[h] = jnp.where(own, 1.0, source[h])
            for i in range(j + 1, PANEL):
                target = list(pair[i])
                target[h] = jnp.where(own, 0.0, target[h])
                pair[i] = [target[c] - ratio[i] * source[c] for c in range(2)]
            row = [source[c] * inv for c in range(2)]
            v = side[j] * inv
            s = [s[c] - v * row[c] for c in range(2)]
            below = [row[0], jnp.zeros_like(row[1])]
            below[h] = jnp.where(at <= o + j, row[h], 0.0)
            q = [q[c] + v * below[c] for c in range(2)]
            vv = vv + v * v
            shown = list(row)
            if h:
                shown[0] = jnp.zeros_like(row[0])
            shown[h] = jnp.where(own, pivot * inv, jnp.where(at > o + j, row[h], 0.0))
            for c in range(2):
                halves[c][rows(base + j), :] = row[c]
                out_ref[rows(base + j), c * LANES : (c + 1) * LANES] = shown[c]
            row[h] = jnp.where((at > o + j) & (at < o + PANEL), 0.0, row[h])
            final.append(row)
        inside = (at >= o) & (at < o + PANEL)

        def group(g, _):
            for i in range(PANEL):
                index = g * PANEL + i
                place = rows(h * LANES + index)
                target = [halves[c][place, :] for c in range(2)]
                target[h] = jnp.where(inside, 0.0, target[h])
                for k in range(PANEL):
                    m = lane(final[k][h], index)
                    target = [target[c] - m * final[k][c] for c in range(2)]
                for c in range(2):
                    halves[c][place, :] = target[c]
            return 0

        lax.fori_loop(p + 1, LANES // PANEL, group, 0)
        return s, q, vv

    zero = jnp.zeros((BINS, LANES), jnp.float32)
    s = [steer_ref[:, c * LANES : (c + 1) * LANES] for c in range(2)]
    carry = (s, [zero, zero], zero)
    carry = lax.fori_loop(0, LANES // PANEL, lambda p, c: panel(0, p, c), carry)

    row_id = lax.broadcasted_iota(jnp.int32, (LANES, LANES), 0)
    col_id = lax.broadcasted_iota(jnp.int32, (LANES, LANES), 1)
    for b in range(BINS):
        top = pl.ds(b, LANES, stride=BINS)
        bottom = pl.ds(LANES * BINS + b, LANES, stride=BINS)
        upper = right[top, :]
        inverse = jnp.where(col_id <= row_id, left[top, :], 0.0)
        across = upper.T
        left[bottom, :] = -jnp.dot(
            across, inverse, precision=lax.Precision.HIGHEST, preferred_element_type=jnp.float32
        )
        right[bottom, :] = right[bottom, :] - jnp.dot(
            across, upper, precision=lax.Precision.HIGHEST, preferred_element_type=jnp.float32
        )

    s, q, vv = lax.fori_loop(0, LANES // PANEL, lambda p, c: panel(1, p, c), carry)
    for c in range(2):
        weight_ref[:, c * LANES : (c + 1) * LANES] = q[c] / vv


def sum_kernel(nx, ny, part_ref, out_ref, slots_x, held, slots_y, sends, arrivals):
    me = lax.axis_index("rng")
    row = lax.axis_index("dop")
    x = me // ny
    y = lax.rem(me, ny)

    def along_x(d):
        return (row, lax.rem(x + d, nx) * ny + y)

    def along_y(d):
        return (row, x * ny + lax.rem(y + d, ny))

    barrier = pltpu.get_barrier_semaphore()
    for d in range(1, nx):
        pl.semaphore_signal(
            barrier, inc=1, device_id=along_x(d), device_id_type=pl.DeviceIdType.MESH
        )
    for d in range(1, ny):
        pl.semaphore_signal(
            barrier, inc=1, device_id=along_y(d), device_id_type=pl.DeviceIdType.MESH
        )
    pl.semaphore_wait(barrier, nx + ny - 2)

    def copy(source, target, stage, d, device):
        return pltpu.make_async_remote_copy(
            src_ref=source,
            dst_ref=target,
            send_sem=sends.at[stage, d],
            recv_sem=arrivals.at[stage, d],
            device_id=device,
            device_id_type=pl.DeviceIdType.MESH,
        )

    def scatter_x(d):
        return copy(part_ref.at[lax.rem(x + d, nx)], slots_x.at[d], 0, d, along_x(d))

    def scatter_y(d):
        return copy(held.at[lax.rem(y + d, ny)], slots_y.at[d], 1, d, along_y(d))

    def gather_y(d, place):
        return copy(out_ref.at[x, place], out_ref.at[x, place], 2, d, along_y(d))

    def gather_x(d, place):
        return copy(out_ref.at[place], out_ref.at[place], 3, d, along_x(d))

    for d in range(1, nx):
        scatter_x(d).start()
    for d in range(1, nx):
        scatter_x(d).wait_recv()
    total = part_ref[x]
    for d in range(1, nx):
        total = total + slots_x[d]
    held[...] = total
    for d in range(1, ny):
        scatter_y(d).start()
    for d in range(1, ny):
        scatter_y(d).wait_recv()
    total = held[y]
    for d in range(1, ny):
        total = total + slots_y[d]
    out_ref[x, y] = total
    for d in range(1, ny):
        gather_y(d, y).start()
    for d in range(1, ny):
        gather_y(d, lax.rem(y + ny - d, ny)).wait_recv()
    for d in range(1, nx):
        gather_x(d, x).start()
    for d in range(1, nx):
        gather_x(d, lax.rem(x + nx - d, nx)).wait_recv()
    for d in range(1, nx):
        scatter_x(d).wait_send()
        gather_x(d, x).wait_send()
    for d in range(1, ny):
        scatter_y(d).wait_send()
        gather_y(d, y).wait_send()


def sum_over_rng(part):
    n = lax.axis_size("rng")
    ny = COLUMN
    nx = n // ny
    chunks = part.reshape(nx, ny, -1, LANES)
    size = chunks.shape[2]
    total = pl.pallas_call(
        functools.partial(sum_kernel, nx, ny),
        out_shape=jax.ShapeDtypeStruct(chunks.shape, jnp.float32),
        in_specs=[pl.BlockSpec(memory_space=pltpu.VMEM)],
        out_specs=pl.BlockSpec(memory_space=pltpu.VMEM),
        scratch_shapes=[
            pltpu.VMEM((nx, ny, size, LANES), jnp.float32),
            pltpu.VMEM((ny, size, LANES), jnp.float32),
            pltpu.VMEM((ny, size, LANES), jnp.float32),
            pltpu.SemaphoreType.DMA((4, ny)),
            pltpu.SemaphoreType.DMA((4, ny)),
        ],
        compiler_params=pltpu.CompilerParams(collective_id=0, has_side_effects=True),
    )(chunks)
    return total.reshape(part.shape)


def factorize(covariance, steering):
    n = covariance.shape[0]
    flat = covariance.reshape(n * BINS, n)
    factor, weight = pl.pallas_call(
        factor_kernel,
        out_shape=(
            jax.ShapeDtypeStruct((n * BINS, n), jnp.float32),
            jax.ShapeDtypeStruct((BINS, n), jnp.float32),
        ),
        in_specs=[pl.BlockSpec(memory_space=pltpu.VMEM)] * 2,
        out_specs=(pl.BlockSpec(memory_space=pltpu.VMEM), pl.BlockSpec(memory_space=pltpu.VMEM)),
        scratch_shapes=[pltpu.VMEM((n * BINS, LANES), jnp.float32)] * 2,
        compiler_params=pltpu.CompilerParams(vmem_limit_bytes=40 * 1024 * 1024),
    )(flat, steering)
    return factor.reshape(n, BINS, n), weight


def shards(cube, train_blocks, guard_blocks, prior_factor, steering):
    rows = prior_factor.shape[1]
    prior = lax.all_gather(prior_factor, "rng", axis=1, tiled=True)
    table = dft_table(cube.shape[2] * lax.axis_size("dop"))
    pulse_block = lax.all_to_all(cube, "dop", split_axis=1, concat_axis=2, tiled=True)
    spectrum = lax.all_to_all(
        spectra(pulse_block, table), "dop", split_axis=2, concat_axis=1, tiled=True
    )
    neighbor = from_behind(spectrum[:, :, 0:1, :], "dop", -1)
    following = jnp.concatenate([spectrum[:, :, 1:, :], neighbor], axis=2)
    vectors = jnp.concatenate([spectrum[0], following[0], spectrum[1], following[1]], axis=0)
    usable = train_blocks * guard_blocks[None, :]
    gate_mask = jnp.repeat(usable, BLOCK, axis=1).astype(jnp.bfloat16)
    masked = vectors * gate_mask[None, :, :]
    half = vectors.shape[0] // 2
    gram = jnp.einsum("dkg,ekg->kde", masked, masked, preferred_element_type=jnp.float32)
    real_part = gram[:, :half, :half] + gram[:, half:, half:]
    cross = gram[:, half:, :half] - gram[:, :half, half:]
    row_id = lax.broadcasted_iota(jnp.int32, (1, half, half), 1)
    col_id = lax.broadcasted_iota(jnp.int32, (1, half, half), 2)
    packed = jnp.where(row_id <= col_id, real_part, cross)
    packed, prior = lax.optimization_barrier((packed, prior))
    prior_gram = forgetting * jnp.einsum(
        "krd,kre->kde", prior, prior, precision=lax.Precision.HIGHEST
    )
    packed = sum_over_rng(packed)
    flipped = jnp.swapaxes(packed, 1, 2)
    real_part = jnp.where(row_id <= col_id, packed, flipped)
    cross = jnp.where(row_id > col_id, packed, jnp.where(row_id < col_id, -flipped, 0.0))
    top = jnp.concatenate([real_part, -cross], axis=2)
    bottom = jnp.concatenate([cross, real_part], axis=2)
    covariance = jnp.concatenate([top, bottom], axis=1) + prior_gram
    upper, weight = factorize(jnp.swapaxes(covariance, 0, 1), steering)
    rotated = jnp.concatenate([-weight[:, half:], weight[:, :half]], axis=1)
    stacked = jnp.stack([weight, rotated]).astype(jnp.bfloat16)
    filtered = jnp.einsum("skd,dkg->skg", stacked, vectors, preferred_element_type=jnp.float32)
    start = lax.axis_index("rng") * rows
    factor = jnp.swapaxes(lax.dynamic_slice_in_dim(upper, start, rows, axis=0), 0, 1)
    return (filtered, factor)


def solution(mesh):
    return jax.shard_map(
        shards,
        mesh=mesh,
        in_specs=(
            P(None, None, "dop", "rng"),
            P("dop", "rng"),
            P("rng"),
            P("dop", "rng", None),
            P("dop", None),
        ),
        out_specs=(P(None, "dop", "rng"), P("dop", "rng", None)),
        check_vma=False,
    )
```

```python
import functools
import math

import jax
import jax.numpy as jnp
from jax import lax
from jax.experimental import pallas as pl
from jax.experimental.pallas import tpu as pltpu
from jax.sharding import PartitionSpec as P

BLOCK = 128
BINS = 8
LANES = 128
PANEL = 8
COLUMN = 8

forgetting = 0.98


def from_behind(block, axis, distance):
    devices = range(lax.axis_size(axis))
    route = [((i - distance) % len(devices), i) for i in devices]
    return lax.ppermute(block, axis, route)


def dft_table(pulses):
    index = jnp.arange(pulses, dtype=jnp.int32)
    product = index[:, None] * index[None, :] % pulses
    angle = product.astype(jnp.float32) * (2.0 * math.pi / pulses)
    cosine = jnp.cos(angle)
    sine = jnp.sin(angle)
    top = jnp.stack([cosine, -sine], axis=1)
    bottom = jnp.stack([sine, cosine], axis=1)
    return jnp.stack([top, bottom], axis=0)


def spectra(pulse_block, table):
    out = jnp.einsum(
        "scpg,sptk->tckg", pulse_block.astype(jnp.float32), table, precision=lax.Precision.HIGHEST
    )
    return out.astype(jnp.bfloat16)


def lane(x, index):
    where = jnp.full((BINS, LANES), index, jnp.int32)
    return jnp.take_along_axis(x, where, axis=1, mode="promise_in_bounds")


def factor_kernel(cov_ref, steer_ref, out_ref, weight_ref, left, right):
    halves = (left, right)
    at = lax.broadcasted_iota(jnp.int32, (BINS, LANES), 1)
    for h in range(2):
        halves[h][...] = cov_ref[:, h * LANES : (h + 1) * LANES]

    def rows(j):
        return pl.ds(pl.multiple_of(j * BINS, BINS), BINS)

    def panel(h, p, carry):
        s, q, vv = carry
        o = p * PANEL
        base = h * LANES + o
        pair = [[halves[c][rows(base + i), :] for c in range(2)] for i in range(PANEL)]
        block = [[lane(pair[j][h], o + i) if i >= j else None for i in range(PANEL)] for j in range(PANEL)]
        side = [lane(s[h], o + j) for j in range(PANEL)]
        final = []
        for j in range(PANEL):
            own = at == o + j
            pivot = block[j][j]
            inv = lax.rsqrt(pivot)
            inv2 = inv * inv
            ratio = [block[j][i] * inv2 if i > j else None for i in range(PANEL)]
            for i in range(j + 1, PANEL):
                for l in range(i, PANEL):
                    block[i][l] = block[i][l] - ratio[i] * block[j][l]
                side[i] = side[i] - ratio[i] * side[j]
            source = list(pair[j])
            source[h] = jnp.where(own, 1.0, source[h])
            for i in range(j + 1, PANEL):
                target = list(pair[i])
                target[h] = jnp.where(own, 0.0, target[h])
                pair[i] = [target[c] - ratio[i] * source[c] for c in range(2)]
            row = [source[c] * inv for c in range(2)]
            v = side[j] * inv
            s = [s[c] - v * row[c] for c in range(2)]
            below = [row[0], jnp.zeros_like(row[1])]
            below[h] = jnp.where(at <= o + j, row[h], 0.0)
            q = [q[c] + v * below[c] for c in range(2)]
            vv = vv + v * v
            shown = list(row)
            if h:
                shown[0] = jnp.zeros_like(row[0])
            shown[h] = jnp.where(own, pivot * inv, jnp.where(at > o + j, row[h], 0.0))
            for c in range(2):
                halves[c][rows(base + j), :] = row[c]
                out_ref[rows(base + j), c * LANES : (c + 1) * LANES] = shown[c]
            row[h] = jnp.where((at > o + j) & (at < o + PANEL), 0.0, row[h])
            final.append(row)
        inside = (at >= o) & (at < o + PANEL)

        def group(g, _):
            for i in range(PANEL):
                index = g * PANEL + i
                place = rows(h * LANES + index)
                target = [halves[c][place, :] for c in range(2)]
                target[h] = jnp.where(inside, 0.0, target[h])
                for k in range(PANEL):
                    m = lane(final[k][h], index)
                    target = [target[c] - m * final[k][c] for c in range(2)]
                for c in range(2):
                    halves[c][place, :] = target[c]
            return 0

        lax.fori_loop(p + 1, LANES // PANEL, group, 0)
        return s, q, vv

    zero = jnp.zeros((BINS, LANES), jnp.float32)
    s = [steer_ref[:, c * LANES : (c + 1) * LANES] for c in range(2)]
    carry = (s, [zero, zero], zero)
    carry = lax.fori_loop(0, LANES // PANEL, lambda p, c: panel(0, p, c), carry)

    row_id = lax.broadcasted_iota(jnp.int32, (LANES, LANES), 0)
    col_id = lax.broadcasted_iota(jnp.int32, (LANES, LANES), 1)
    for b in range(BINS):
        top = pl.ds(b, LANES, stride=BINS)
        bottom = pl.ds(LANES * BINS + b, LANES, stride=BINS)
        upper = right[top, :]
        inverse = jnp.where(col_id <= row_id, left[top, :], 0.0)
        across = upper.T
        left[bottom, :] = -jnp.dot(
            across, inverse, precision=lax.Precision.HIGHEST, preferred_element_type=jnp.float32
        )
        right[bottom, :] = right[bottom, :] - jnp.dot(
            across, upper, precision=lax.Precision.HIGHEST, preferred_element_type=jnp.float32
        )

    s, q, vv = lax.fori_loop(0, LANES // PANEL, lambda p, c: panel(1, p, c), carry)
    for c in range(2):
        weight_ref[:, c * LANES : (c + 1) * LANES] = q[c] / vv


def sum_kernel(nx, ny, part_ref, out_ref, slots_x, held, slots_y, sends, arrivals):
    me = lax.axis_index("rng")
    row = lax.axis_index("dop")
    x = me // ny
    y = lax.rem(me, ny)

    def along_x(d):
        return (row, lax.rem(x + d, nx) * ny + y)

    def along_y(d):
        return (row, x * ny + lax.rem(y + d, ny))

    barrier = pltpu.get_barrier_semaphore()
    for d in range(1, nx):
        pl.semaphore_signal(
            barrier, inc=1, device_id=along_x(d), device_id_type=pl.DeviceIdType.MESH
        )
    for d in range(1, ny):
        pl.semaphore_signal(
            barrier, inc=1, device_id=along_y(d), device_id_type=pl.DeviceIdType.MESH
        )
    pl.semaphore_wait(barrier, nx + ny - 2)

    def copy(source, target, stage, d, device):
        return pltpu.make_async_remote_copy(
            src_ref=source,
            dst_ref=target,
            send_sem=sends.at[stage, d],
            recv_sem=arrivals.at[stage, d],
            device_id=device,
            device_id_type=pl.DeviceIdType.MESH,
        )

    def scatter_x(d):
        return copy(part_ref.at[lax.rem(x + d, nx)], slots_x.at[d], 0, d, along_x(d))

    def scatter_y(d):
        return copy(held.at[lax.rem(y + d, ny)], slots_y.at[d], 1, d, along_y(d))

    def gather_y(d, place):
        return copy(out_ref.at[x, place], out_ref.at[x, place], 2, d, along_y(d))

    def gather_x(d, place):
        return copy(out_ref.at[place], out_ref.at[place], 3, d, along_x(d))

    for d in range(1, nx):
        scatter_x(d).start()
    for d in range(1, nx):
        scatter_x(d).wait_recv()
    total = part_ref[x]
    for d in range(1, nx):
        total = total + slots_x[d]
    held[...] = total
    for d in range(1, ny):
        scatter_y(d).start()
    for d in range(1, ny):
        scatter_y(d).wait_recv()
    total = held[y]
    for d in range(1, ny):
        total = total + slots_y[d]
    out_ref[x, y] = total
    for d in range(1, ny):
        gather_y(d, y).start()
    for d in range(1, ny):
        gather_y(d, lax.rem(y + ny - d, ny)).wait_recv()
    for d in range(1, nx):
        gather_x(d, x).start()
    for d in range(1, nx):
        gather_x(d, lax.rem(x + nx - d, nx)).wait_recv()
    for d in range(1, nx):
        scatter_x(d).wait_send()
        gather_x(d, x).wait_send()
    for d in range(1, ny):
        scatter_y(d).wait_send()
        gather_y(d, y).wait_send()


def sum_over_rng(part):
    n = lax.axis_size("rng")
    ny = COLUMN
    nx = n // ny
    chunks = part.reshape(nx, ny, -1, LANES)
    size = chunks.shape[2]
    total = pl.pallas_call(
        functools.partial(sum_kernel, nx, ny),
        out_shape=jax.ShapeDtypeStruct(chunks.shape, jnp.float32),
        in_specs=[pl.BlockSpec(memory_space=pltpu.VMEM)],
        out_specs=pl.BlockSpec(memory_space=pltpu.VMEM),
        scratch_shapes=[
            pltpu.VMEM((nx, ny, size, LANES), jnp.float32),
            pltpu.VMEM((ny, size, LANES), jnp.float32),
            pltpu.VMEM((ny, size, LANES), jnp.float32),
            pltpu.SemaphoreType.DMA((4, ny)),
            pltpu.SemaphoreType.DMA((4, ny)),
        ],
        compiler_params=pltpu.CompilerParams(collective_id=0, has_side_effects=True),
    )(chunks)
    return total.reshape(part.shape)


def factorize(covariance, steering):
    n = covariance.shape[0]
    flat = covariance.reshape(n * BINS, n)
    factor, weight = pl.pallas_call(
        factor_kernel,
        out_shape=(
            jax.ShapeDtypeStruct((n * BINS, n), jnp.float32),
            jax.ShapeDtypeStruct((BINS, n), jnp.float32),
        ),
        in_specs=[pl.BlockSpec(memory_space=pltpu.VMEM)] * 2,
        out_specs=(pl.BlockSpec(memory_space=pltpu.VMEM), pl.BlockSpec(memory_space=pltpu.VMEM)),
        scratch_shapes=[pltpu.VMEM((n * BINS, LANES), jnp.float32)] * 2,
        compiler_params=pltpu.CompilerParams(vmem_limit_bytes=40 * 1024 * 1024),
    )(flat, steering)
    return factor.reshape(n, BINS, n), weight


def shards(cube, train_blocks, guard_blocks, prior_factor, steering):
    rows = prior_factor.shape[1]
    prior = lax.all_gather(prior_factor, "rng", axis=1, tiled=True)
    table = dft_table(cube.shape[2] * lax.axis_size("dop"))
    pulse_block = lax.all_to_all(cube, "dop", split_axis=1, concat_axis=2, tiled=True)
    spectrum = lax.all_to_all(
        spectra(pulse_block, table), "dop", split_axis=2, concat_axis=1, tiled=True
    )
    neighbor = from_behind(spectrum[:, :, 0:1, :], "dop", -1)
    following = jnp.concatenate([spectrum[:, :, 1:, :], neighbor], axis=2)
    vectors = jnp.concatenate([spectrum[0], following[0], spectrum[1], following[1]], axis=0)
    usable = train_blocks * guard_blocks[None, :]
    gate_mask = jnp.repeat(usable, BLOCK, axis=1).astype(jnp.bfloat16)
    masked = vectors * gate_mask[None, :, :]
    half = vectors.shape[0] // 2
    gram = jnp.einsum("dkg,ekg->kde", masked, masked, preferred_element_type=jnp.float32)
    real_part = gram[:, :half, :half] + gram[:, half:, half:]
    cross = gram[:, half:, :half] - gram[:, :half, half:]
    row_id = lax.broadcasted_iota(jnp.int32, (1, half, half), 1)
    col_id = lax.broadcasted_iota(jnp.int32, (1, half, half), 2)
    packed = sum_over_rng(jnp.where(row_id <= col_id, real_part, cross))
    packed, prior = lax.optimization_barrier((packed, prior))
    prior_gram = forgetting * jnp.einsum(
        "krd,kre->kde", prior, prior, precision=lax.Precision.HIGHEST
    )
    flipped = jnp.swapaxes(packed, 1, 2)
    real_part = jnp.where(row_id <= col_id, packed, flipped)
    cross = jnp.where(row_id > col_id, packed, jnp.where(row_id < col_id, -flipped, 0.0))
    top = jnp.concatenate([real_part, -cross], axis=2)
    bottom = jnp.concatenate([cross, real_part], axis=2)
    covariance = jnp.concatenate([top, bottom], axis=1) + prior_gram
    upper, weight = factorize(jnp.swapaxes(covariance, 0, 1), steering)
    rotated = jnp.concatenate([-weight[:, half:], weight[:, :half]], axis=1)
    stacked = jnp.stack([weight, rotated]).astype(jnp.bfloat16)
    filtered = jnp.einsum("skd,dkg->skg", stacked, vectors, preferred_element_type=jnp.float32)
    start = lax.axis_index("rng") * rows
    factor = jnp.swapaxes(lax.dynamic_slice_in_dim(upper, start, rows, axis=0), 0, 1)
    return (filtered, factor)


def solution(mesh):
    return jax.shard_map(
        shards,
        mesh=mesh,
        in_specs=(
            P(None, None, "dop", "rng"),
            P("dop", "rng"),
            P("rng"),
            P("dop", "rng", None),
            P("dop", None),
        ),
        out_specs=(P(None, "dop", "rng"), P("dop", "rng", None)),
        check_vma=False,
    )
```

```python
import functools
import math

import jax
import jax.numpy as jnp
from jax import lax
from jax.experimental import pallas as pl
from jax.experimental.pallas import tpu as pltpu
from jax.sharding import PartitionSpec as P

BLOCK = 128
BINS = 8
LANES = 128
PANEL = 8
COLUMN = 8

forgetting = 0.98


def from_behind(block, axis, distance):
    devices = range(lax.axis_size(axis))
    route = [((i - distance) % len(devices), i) for i in devices]
    return lax.ppermute(block, axis, route)


def dft_table(pulses):
    index = jnp.arange(pulses, dtype=jnp.int32)
    product = index[:, None] * index[None, :] % pulses
    angle = product.astype(jnp.float32) * (2.0 * math.pi / pulses)
    cosine = jnp.cos(angle)
    sine = jnp.sin(angle)
    top = jnp.stack([cosine, -sine], axis=1)
    bottom = jnp.stack([sine, cosine], axis=1)
    return jnp.stack([top, bottom], axis=0)


def spectra(pulse_block, table):
    out = jnp.einsum(
        "scpg,sptk->tckg", pulse_block.astype(jnp.float32), table, precision=lax.Precision.HIGHEST
    )
    return out.astype(jnp.bfloat16)


def lane(x, index):
    where = jnp.full((BINS, LANES), index, jnp.int32)
    return jnp.take_along_axis(x, where, axis=1, mode="promise_in_bounds")


def factor_kernel(cov_ref, steer_ref, out_ref, weight_ref, left, right):
    halves = (left, right)
    at = lax.broadcasted_iota(jnp.int32, (BINS, LANES), 1)
    for h in range(2):
        halves[h][...] = cov_ref[:, h * LANES : (h + 1) * LANES]

    def rows(j):
        return pl.ds(pl.multiple_of(j * BINS, BINS), BINS)

    def panel(h, p, carry):
        s, q, vv = carry
        o = p * PANEL
        base = h * LANES + o
        pair = [[halves[c][rows(base + i), :] for c in range(2)] for i in range(PANEL)]
        block = [[lane(pair[j][h], o + i) if i >= j else None for i in range(PANEL)] for j in range(PANEL)]
        side = [lane(s[h], o + j) for j in range(PANEL)]
        final = []
        for j in range(PANEL):
            own = at == o + j
            pivot = block[j][j]
            inv = lax.rsqrt(pivot)
            inv2 = inv * inv
            ratio = [block[j][i] * inv2 if i > j else None for i in range(PANEL)]
            for i in range(j + 1, PANEL):
                for l in range(i, PANEL):
                    block[i][l] = block[i][l] - ratio[i] * block[j][l]
                side[i] = side[i] - ratio[i] * side[j]
            source = list(pair[j])
            source[h] = jnp.where(own, 1.0, source[h])
            for i in range(j + 1, PANEL):
                target = list(pair[i])
                target[h] = jnp.where(own, 0.0, target[h])
                pair[i] = [target[c] - ratio[i] * source[c] for c in range(2)]
            row = [source[c] * inv for c in range(2)]
            v = side[j] * inv
            s = [s[c] - v * row[c] for c in range(2)]
            below = [row[0], jnp.zeros_like(row[1])]
            below[h] = jnp.where(at <= o + j, row[h], 0.0)
            q = [q[c] + v * below[c] for c in range(2)]
            vv = vv + v * v
            shown = list(row)
            if h:
                shown[0] = jnp.zeros_like(row[0])
            shown[h] = jnp.where(own, pivot * inv, jnp.where(at > o + j, row[h], 0.0))
            for c in range(2):
                halves[c][rows(base + j), :] = row[c]
                out_ref[rows(base + j), c * LANES : (c + 1) * LANES] = shown[c]
            row[h] = jnp.where((at > o + j) & (at < o + PANEL), 0.0, row[h])
            final.append(row)
        inside = (at >= o) & (at < o + PANEL)

        def group(g, _):
            for i in range(PANEL):
                index = g * PANEL + i
                place = rows(h * LANES + index)
                target = [halves[c][place, :] for c in range(2)]
                target[h] = jnp.where(inside, 0.0, target[h])
                for k in range(PANEL):
                    m = lane(final[k][h], index)
                    target = [target[c] - m * final[k][c] for c in range(2)]
                for c in range(2):
                    halves[c][place, :] = target[c]
            return 0

        lax.fori_loop(p + 1, LANES // PANEL, group, 0)
        return s, q, vv

    zero = jnp.zeros((BINS, LANES), jnp.float32)
    s = [steer_ref[:, c * LANES : (c + 1) * LANES] for c in range(2)]
    carry = (s, [zero, zero], zero)
    carry = lax.fori_loop(0, LANES // PANEL, lambda p, c: panel(0, p, c), carry)

    row_id = lax.broadcasted_iota(jnp.int32, (LANES, LANES), 0)
    col_id = lax.broadcasted_iota(jnp.int32, (LANES, LANES), 1)
    for b in range(BINS):
        top = pl.ds(b, LANES, stride=BINS)
        bottom = pl.ds(LANES * BINS + b, LANES, stride=BINS)
        upper = right[top, :]
        inverse = jnp.where(col_id <= row_id, left[top, :], 0.0)
        both = jnp.dot(
            upper.T,
            jnp.concatenate([inverse, upper], axis=1),
            precision=lax.Precision.HIGHEST,
            preferred_element_type=jnp.float32,
        )
        left[bottom, :] = -both[:, :LANES]
        right[bottom, :] = right[bottom, :] - both[:, LANES:]

    s, q, vv = lax.fori_loop(0, LANES // PANEL, lambda p, c: panel(1, p, c), carry)
    for c in range(2):
        weight_ref[:, c * LANES : (c + 1) * LANES] = q[c] / vv


def sum_kernel(nx, ny, part_ref, out_ref, slots_x, held, slots_y, sends, arrivals):
    me = lax.axis_index("rng")
    row = lax.axis_index("dop")
    x = me // ny
    y = lax.rem(me, ny)

    def along_x(d):
        return (row, lax.rem(x + d, nx) * ny + y)

    def along_y(d):
        return (row, x * ny + lax.rem(y + d, ny))

    barrier = pltpu.get_barrier_semaphore()
    for d in range(1, nx):
        pl.semaphore_signal(
            barrier, inc=1, device_id=along_x(d), device_id_type=pl.DeviceIdType.MESH
        )
    for d in range(1, ny):
        pl.semaphore_signal(
            barrier, inc=1, device_id=along_y(d), device_id_type=pl.DeviceIdType.MESH
        )
    pl.semaphore_wait(barrier, nx + ny - 2)

    def copy(source, target, stage, d, device):
        return pltpu.make_async_remote_copy(
            src_ref=source,
            dst_ref=target,
            send_sem=sends.at[stage, d],
            recv_sem=arrivals.at[stage, d],
            device_id=device,
            device_id_type=pl.DeviceIdType.MESH,
        )

    def scatter_x(d):
        return copy(part_ref.at[lax.rem(x + d, nx)], slots_x.at[d], 0, d, along_x(d))

    def scatter_y(d):
        return copy(held.at[lax.rem(y + d, ny)], slots_y.at[d], 1, d, along_y(d))

    def gather_y(d, place):
        return copy(out_ref.at[x, place], out_ref.at[x, place], 2, d, along_y(d))

    def gather_x(d, place):
        return copy(out_ref.at[place], out_ref.at[place], 3, d, along_x(d))

    for d in range(1, nx):
        scatter_x(d).start()
    for d in range(1, nx):
        scatter_x(d).wait_recv()
    total = part_ref[x]
    for d in range(1, nx):
        total = total + slots_x[d]
    held[...] = total
    for d in range(1, ny):
        scatter_y(d).start()
    for d in range(1, ny):
        scatter_y(d).wait_recv()
    total = held[y]
    for d in range(1, ny):
        total = total + slots_y[d]
    out_ref[x, y] = total
    for d in range(1, ny):
        gather_y(d, y).start()
    for d in range(1, ny):
        gather_y(d, lax.rem(y + ny - d, ny)).wait_recv()
    for d in range(1, nx):
        gather_x(d, x).start()
    for d in range(1, nx):
        gather_x(d, lax.rem(x + nx - d, nx)).wait_recv()
    for d in range(1, nx):
        scatter_x(d).wait_send()
        gather_x(d, x).wait_send()
    for d in range(1, ny):
        scatter_y(d).wait_send()
        gather_y(d, y).wait_send()


def sum_over_rng(part):
    n = lax.axis_size("rng")
    ny = COLUMN
    nx = n // ny
    chunks = part.reshape(nx, ny, -1, LANES)
    size = chunks.shape[2]
    total = pl.pallas_call(
        functools.partial(sum_kernel, nx, ny),
        out_shape=jax.ShapeDtypeStruct(chunks.shape, jnp.float32),
        in_specs=[pl.BlockSpec(memory_space=pltpu.VMEM)],
        out_specs=pl.BlockSpec(memory_space=pltpu.VMEM),
        scratch_shapes=[
            pltpu.VMEM((nx, ny, size, LANES), jnp.float32),
            pltpu.VMEM((ny, size, LANES), jnp.float32),
            pltpu.VMEM((ny, size, LANES), jnp.float32),
            pltpu.SemaphoreType.DMA((4, ny)),
            pltpu.SemaphoreType.DMA((4, ny)),
        ],
        compiler_params=pltpu.CompilerParams(collective_id=0, has_side_effects=True),
    )(chunks)
    return total.reshape(part.shape)


def factorize(covariance, steering):
    n = covariance.shape[0]
    flat = covariance.reshape(n * BINS, n)
    factor, weight = pl.pallas_call(
        factor_kernel,
        out_shape=(
            jax.ShapeDtypeStruct((n * BINS, n), jnp.float32),
            jax.ShapeDtypeStruct((BINS, n), jnp.float32),
        ),
        in_specs=[pl.BlockSpec(memory_space=pltpu.VMEM)] * 2,
        out_specs=(pl.BlockSpec(memory_space=pltpu.VMEM), pl.BlockSpec(memory_space=pltpu.VMEM)),
        scratch_shapes=[pltpu.VMEM((n * BINS, LANES), jnp.float32)] * 2,
        compiler_params=pltpu.CompilerParams(vmem_limit_bytes=40 * 1024 * 1024),
    )(flat, steering)
    return factor.reshape(n, BINS, n), weight


def shards(cube, train_blocks, guard_blocks, prior_factor, steering):
    rows = prior_factor.shape[1]
    prior = lax.all_gather(prior_factor, "rng", axis=1, tiled=True)
    table = dft_table(cube.shape[2] * lax.axis_size("dop"))
    pulse_block = lax.all_to_all(cube, "dop", split_axis=1, concat_axis=2, tiled=True)
    spectrum = lax.all_to_all(
        spectra(pulse_block, table), "dop", split_axis=2, concat_axis=1, tiled=True
    )
    neighbor = from_behind(spectrum[:, :, 0:1, :], "dop", -1)
    following = jnp.concatenate([spectrum[:, :, 1:, :], neighbor], axis=2)
    vectors = jnp.concatenate([spectrum[0], following[0], spectrum[1], following[1]], axis=0)
    usable = train_blocks * guard_blocks[None, :]
    gate_mask = jnp.repeat(usable, BLOCK, axis=1).astype(jnp.bfloat16)
    masked = vectors * gate_mask[None, :, :]
    half = vectors.shape[0] // 2
    gram = jnp.einsum("dkg,ekg->kde", masked, masked, preferred_element_type=jnp.float32)
    real_part = gram[:, :half, :half] + gram[:, half:, half:]
    cross = gram[:, half:, :half] - gram[:, :half, half:]
    row_id = lax.broadcasted_iota(jnp.int32, (1, half, half), 1)
    col_id = lax.broadcasted_iota(jnp.int32, (1, half, half), 2)
    packed = sum_over_rng(jnp.where(row_id <= col_id, real_part, cross))
    packed, prior = lax.optimization_barrier((packed, prior))
    prior_gram = forgetting * jnp.einsum(
        "krd,kre->kde", prior, prior, precision=lax.Precision.HIGHEST
    )
    flipped = jnp.swapaxes(packed, 1, 2)
    real_part = jnp.where(row_id <= col_id, packed, flipped)
    cross = jnp.where(row_id > col_id, packed, jnp.where(row_id < col_id, -flipped, 0.0))
    top = jnp.concatenate([real_part, -cross], axis=2)
    bottom = jnp.concatenate([cross, real_part], axis=2)
    covariance = jnp.concatenate([top, bottom], axis=1) + prior_gram
    upper, weight = factorize(jnp.swapaxes(covariance, 0, 1), steering)
    rotated = jnp.concatenate([-weight[:, half:], weight[:, :half]], axis=1)
    stacked = jnp.stack([weight, rotated]).astype(jnp.bfloat16)
    filtered = jnp.einsum("skd,dkg->skg", stacked, vectors, preferred_element_type=jnp.float32)
    start = lax.axis_index("rng") * rows
    factor = jnp.swapaxes(lax.dynamic_slice_in_dim(upper, start, rows, axis=0), 0, 1)
    return (filtered, factor)


def solution(mesh):
    return jax.shard_map(
        shards,
        mesh=mesh,
        in_specs=(
            P(None, None, "dop", "rng"),
            P("dop", "rng"),
            P("rng"),
            P("dop", "rng", None),
            P("dop", None),
        ),
        out_specs=(P(None, "dop", "rng"), P("dop", "rng", None)),
        check_vma=False,
    )
```
